1024 devices in a mesh: rows: 128 (over z, y), cols: 8 (over x, core).
Axes of the slice: x: 4, y: 8, z: 16, core: 2. Of those that a mesh axis runs over, the one named last changes fastest.
Arguments:
- z_blocks: float32 [512, 8, 256, 256], P('rows', 'cols'), may hold values from -0.125 to 0.125
- z_cols: int32 [512, 8], P('rows', 'cols'), may hold values from 0 to 511, as said below
- z_count: int32 [512], P('rows'), may hold values from 2 to 8, as said below
- h_blocks: float32 [512, 8, 256, 256], P('rows', 'cols'), may hold values from -0.125 to 0.125
- h_cols: int32 [512, 8], P('rows', 'cols'), may hold values from 0 to 511, as said below
- h_count: int32 [512], P('rows'), may hold values from 2 to 8, as said below
- panel: float32 [512, 256, 64], P('rows'), may hold values from -6 to 6
Outputs:
- result: float32 [512, 256, 64], P('rows', 'cols')
The draws below stay inside these ranges and needn't reach their ends.
Inputs may be any that keep to these rules, and one draw needn't show every extreme that they name: `z_cols`: within a block row the column block indices of the slots are distinct; block row i only names blocks from 4 * (i // 4) - 4 to 4 * (i // 4) + 7. `h_cols`: same law as z_cols, drawn apart. `z_count`: block row 0 uses all 8 slots. `h_count`: block row 0 uses all 8 slots.
All inputs are finite; a program needn't handle non-finite values.
Results may differ from the reference program's by a relative error of at most 0.000098.
Values sent between devices are 32-bit elements; how exact they have to be, the bound alone decides.
No kernel may reach another device: no remote copies, remote signals or barrier semaphores. Data moves between devices by JAX's collectives and lax.ppermute only.
A program may use at most 32 MiB of HBM per device.

```python
import jax
import jax.numpy as jnp
from jax import lax

BLK = 256
P_SIZE = 64
R = 4
HB = 4
KS = 8
NB = 512
WB = 12


def band_pattern(key):
    rowids = jnp.arange(NB, dtype=jnp.int32)
    lower = rowids // R * R - HB
    offsets = jnp.arange(WB, dtype=jnp.int32)
    global_cols = lower[:, None] + offsets[None, :]
    valid = (global_cols >= 0) & (global_cols < NB)
    score = jax.random.randint(key, (NB, WB), 0, 4096, dtype=jnp.int32) * WB + offsets[None, :]
    score = score + jnp.where(valid, 0, 8192 * WB)
    order = jnp.argsort(score, axis=1, stable=True)[:, :KS]
    return jnp.take_along_axis(global_cols, order, axis=1).astype(jnp.int32)


def slot_counts(key):
    counts = jax.random.randint(key, (NB,), KS // 4, KS + 1, dtype=jnp.int32)
    return jnp.where(jnp.arange(NB) == 0, KS, counts).astype(jnp.int32)


def draw_z_cols(key, part):
    return band_pattern(jax.random.fold_in(key, 11))


def draw_h_cols(key, part):
    return band_pattern(jax.random.fold_in(key, 23))


def draw_z_count(key, part):
    return slot_counts(jax.random.fold_in(key, 37))


def draw_h_count(key, part):
    return slot_counts(jax.random.fold_in(key, 41))


def steps_of(stream_key, dims, pieces, least, high):
    loudness = 1.0
    for position, blocks in pieces:
        heights = jax.random.uniform(jax.random.fold_in(jax.random.fold_in(stream_key, 6), position), (blocks,), jnp.float32, least / len(pieces), high / len(pieces))
        loudness = loudness * jnp.repeat(jnp.exp(heights), dims[position] // blocks).reshape((-1,) + (1,) * (len(dims) - 1 - position))
    return loudness


def normal_values(rng, extent, deviation, bound, cuts=(), kind=jnp.bfloat16):
    factor_of = steps_of(rng, extent, cuts, -0.22, 0.18) if cuts else 1.0
    result = jax.random.normal(rng, extent, jnp.float32) * deviation * factor_of
    return jnp.minimum(jnp.maximum(result, -bound), bound).astype(kind)


def setup_inputs(seed: int = 0) -> dict:
    splits = jax.random.split(jax.random.key(seed), 8)
    return {
        "z_blocks": normal_values(splits[0], (NB, KS, BLK, BLK), (KS * BLK) ** -0.5, 0.125, ((0, 128), (1, 8)), jnp.float32),
        "z_cols": draw_z_cols(jax.random.fold_in(splits[7], 71), 0),
        "z_count": draw_z_count(jax.random.fold_in(splits[7], 71), 0),
        "h_blocks": normal_values(splits[3], (NB, KS, BLK, BLK), (KS * BLK) ** -0.5, 0.125, ((0, 128), (1, 8)), jnp.float32),
        "h_cols": draw_h_cols(jax.random.fold_in(splits[7], 71), 0),
        "h_count": draw_h_count(jax.random.fold_in(splits[7], 71), 0),
        "panel": normal_values(splits[6], (NB, BLK, P_SIZE), 1.0, 6.0, ((0, 128),), jnp.float32),
    }


def used_mask(count):
    return (jnp.arange(KS)[None, :] < count[:, None]).astype(jnp.float32)


def apply_rows(blocks, cols, count, field):
    picked = field[cols] * used_mask(count)[:, :, None, None]
    return jnp.einsum('ikpq,ikqn->ipn', blocks, picked, precision=lax.Precision.HIGHEST)


def reference(z_blocks, z_cols, z_count, h_blocks, h_cols, h_count, panel):
    mid = apply_rows(z_blocks, z_cols, z_count, panel)
    side = apply_rows(h_blocks, h_cols, h_count, mid)
    terms = jnp.einsum('ikqp,iqn->ikpn', z_blocks, side, precision=lax.Precision.HIGHEST)
    terms = terms * used_mask(z_count)[:, :, None, None]
    flat = terms.reshape(NB * KS, BLK, P_SIZE)
    return jax.ops.segment_sum(flat, z_cols.reshape(-1), num_segments=NB)
```

```python
import jax
import jax.numpy as jnp
from jax import lax
from jax.experimental import pallas as pl
from jax.experimental.pallas import tpu as pltpu
from jax.sharding import Mesh, PartitionSpec as P


HB = 4
VMEM = pl.BlockSpec(memory_space=pltpu.VMEM)


def split(x):
    high = x.astype(jnp.bfloat16)
    low = (x - high.astype(jnp.float32)).astype(jnp.bfloat16)
    return high, low


def product(x, block, dims):
    m = x.shape[0]
    xh, xl = split(x)
    bh, bl = split(block)
    dot = lambda a, b: lax.dot_general(a, b, (dims, ((), ())), preferred_element_type=jnp.float32)
    both = dot(jnp.concatenate([xh, xl], axis=0), bh)
    return both[:m] + (both[m:] + dot(xh, bl))


def pick(fields, index):
    picked = jnp.zeros(fields[0].shape, jnp.float32)
    for w, field in enumerate(fields):
        picked = jnp.where(index == w, field, picked)
    return picked


def forward_kernel(row, low, own, high, mine, theirs, index_mine, index_theirs, out):
    n = own.shape[1]
    fields = [ref[j] for ref in (low, own, high) for j in range(HB)]
    for i in range(HB):
        total = None
        for blocks, index in ((mine, index_mine), (theirs, index_theirs)):
            where = jnp.broadcast_to(index[pl.ds(index.shape[0] - 8 + row + i, 1), :], (n, 256))
            part = product(pick(fields, where), blocks[pl.ds(i * 256, 256), :], ((1,), (1,)))
            total = part if total is None else total + part
        for x in range(out.shape[0]):
            out[x, i] = total


def backward_kernel(parts, mine, theirs, index_mine, index_theirs, low, own, high):
    n = own.shape[1]
    outs = [(ref, j) for ref in (low, own, high) for j in range(HB)]
    for ref, j in outs:
        ref[j] = jnp.zeros((n, 256), jnp.float32)
    for i in range(HB):
        side = (parts[0, i] + parts[1, i]) + (parts[2, i] + parts[3, i])
        for blocks, index in ((mine, index_mine), (theirs, index_theirs)):
            where = jnp.broadcast_to(index[pl.ds(index.shape[0] - 8 + i, 1), :], (n, 256))
            term = product(side, blocks[pl.ds(i * 256, 256), :], ((1,), (0,)))
            for w, (ref, j) in enumerate(outs):
                ref[j] = ref[j] + jnp.where(where == w, term, 0.0)


def pack_kernel(own, below, above, out):
    for t in range(2):
        for j in range(HB):
            total = (
                own[j, :, pl.ds(128 * t, 128)]
                + below[j, :, pl.ds(128 * t, 128)]
                + above[j, :, pl.ds(128 * t, 128)]
            )
            for u in range(4):
                shift = (32 * (j - u)) % 128
                turned = total if shift == 0 else pltpu.roll(total, shift, 1)
                out[4 * t + u, :, pl.ds(32 * j, 32)] = turned[:, 32 * j : 32 * j + 32]


def final_kernel(parts, out):
    halves = []
    for q in range(2):
        halves.append((parts[q] + parts[2 + q]) + (parts[4 + q] + parts[6 + q]))
    total = jnp.concatenate(halves + halves, axis=0)
    out[...] = jnp.transpose(total)[:, :64].reshape(out.shape)


def call(kernel, out_shape, count, flops, size):
    return pl.pallas_call(
        kernel,
        out_shape=out_shape,
        in_specs=[VMEM] * count,
        out_specs=jax.tree.map(lambda _: VMEM, out_shape),
        cost_estimate=pl.CostEstimate(flops=flops, bytes_accessed=size, transcendentals=0),
        compiler_params=pltpu.CompilerParams(vmem_limit_bytes=8 << 20),
    )


def f32(*shape):
    return jax.ShapeDtypeStruct(shape, jnp.float32)


def neighbours(up, down):
    count = lax.axis_size("rows")
    below = lax.ppermute(up, "rows", [(i, i + 1) for i in range(count - 1)])
    above = lax.ppermute(down, "rows", [(i + 1, i) for i in range(count - 1)])
    return below, above


def steps(z_blocks, z_cols, z_count, h_blocks, h_cols, h_count, panel):
    q = lax.axis_index("core")
    slot = lax.axis_index("x") * 2 + q
    start = lax.axis_index("rows") * HB - HB
    z = z_blocks.reshape(1024, 256)
    h = h_blocks.reshape(1024, 256)

    def index_rows(cols, count):
        return jnp.where(slot < count, cols[:, 0] - start, -1)

    index = jnp.concatenate([index_rows(z_cols, z_count), index_rows(h_cols, h_count)])
    index = jnp.broadcast_to(index.astype(jnp.float32)[:, None], (8, 256))

    swap = [(0, 1), (1, 0)]
    x = lax.dynamic_slice_in_dim(jnp.swapaxes(panel, 1, 2), q * 32, 32, axis=1)
    x_low, x_high = neighbours(x, x)
    theirs = lax.ppermute(jnp.concatenate([z, index], axis=0), "core", swap)
    h_theirs = lax.ppermute(h, "core", swap)

    def forward(row, low, own, high, mine, other):
        body = lambda *refs: forward_kernel(row, *refs)
        return call(body, f32(4, HB, 32, 256), 7, 1 << 28, 1 << 22)(low, own, high, mine, other, index, theirs)

    def exchange(parts):
        return lax.all_to_all(parts, "x", 0, 0, tiled=True)

    mid = exchange(forward(0, x_low, x, x_high, z, theirs)).sum(axis=0)
    mid_low, mid_high = neighbours(mid, mid)
    side = exchange(forward(4, mid_low, mid, mid_high, h, h_theirs))
    shape = f32(HB, 32, 256)
    low, own, high = call(backward_kernel, (shape, shape, shape), 5, 1 << 28, 1 << 22)(
        side, z, theirs, index, theirs
    )
    from_below, from_above = neighbours(high, low)
    packed = call(pack_kernel, f32(8, 32, 128), 3, 1 << 20, 1 << 20)(own, from_below, from_above)
    arrived = lax.all_to_all(packed, ("x", "core"), 0, 0, tiled=True)
    return call(final_kernel, f32(HB, 32, 64), 1, 1 << 20, 1 << 18)(arrived)


def solution(mesh):
    grid = Mesh(mesh.devices.reshape(mesh.shape["rows"], 4, 2), ("rows", "x", "core"))
    cols = ("x", "core")
    return jax.shard_map(
        steps,
        mesh=grid,
        in_specs=(
            P("rows", cols, None, None),
            P("rows", cols),
            P("rows"),
            P("rows", cols, None, None),
            P("rows", cols),
            P("rows"),
            P("rows", None, None),
        ),
        out_specs=P("rows", cols, None),
        check_vma=False,
    )
```

```python
import jax
import jax.numpy as jnp
from jax import lax
from jax.experimental import pallas as pl
from jax.experimental.pallas import tpu as pltpu
from jax.sharding import Mesh, PartitionSpec as P


HB = 4
VMEM = pl.BlockSpec(memory_space=pltpu.VMEM)


def split(x):
    high = x.astype(jnp.bfloat16)
    low = (x - high.astype(jnp.float32)).astype(jnp.bfloat16)
    return high, low


def product(x, block, dims):
    m = x.shape[0]
    xh, xl = split(x)
    bh, bl = split(block)
    dot = lambda a, b: lax.dot_general(a, b, (dims, ((), ())), preferred_element_type=jnp.float32)
    both = dot(jnp.concatenate([xh, xl], axis=0), bh)
    return both[:m] + (both[m:] + dot(xh, bl))


def pick(fields, index):
    picked = jnp.zeros(fields[0].shape, jnp.float32)
    for w, field in enumerate(fields):
        picked = jnp.where(index == w, field, picked)
    return picked


def forward_kernel(row, low, own, high, mine, theirs, index_mine, index_theirs, out):
    n = own.shape[1]
    fields = [ref[j] for ref in (low, own, high) for j in range(HB)]
    for i in range(HB):
        total = None
        for blocks, index in ((mine, index_mine), (theirs, index_theirs)):
            where = jnp.broadcast_to(index[pl.ds(index.shape[0] - 8 + row + i, 1), :], (n, 256))
            part = product(pick(fields, where), blocks[pl.ds(i * 256, 256), :], ((1,), (1,)))
            total = part if total is None else total + part
        for x in range(out.shape[0]):
            out[x, i] = total


def backward_kernel(parts, mine, theirs, index_mine, index_theirs, low, own, high):
    n = own.shape[1]
    outs = [(ref, j) for ref in (low, own, high) for j in range(HB)]
    for ref, j in outs:
        ref[j] = jnp.zeros((n, 256), jnp.float32)
    for i in range(HB):
        side = (parts[0, i] + parts[1, i]) + (parts[2, i] + parts[3, i])
        for blocks, index in ((mine, index_mine), (theirs, index_theirs)):
            where = jnp.broadcast_to(index[pl.ds(index.shape[0] - 8 + i, 1), :], (n, 256))
            term = product(side, blocks[pl.ds(i * 256, 256), :], ((1,), (0,)))
            for w, (ref, j) in enumerate(outs):
                ref[j] = ref[j] + jnp.where(where == w, term, 0.0)


def fold_kernel(parts, out):
    out[...] = (parts[0] + parts[1]) + (parts[2] + parts[3])


def stage_kernel(*refs):
    *small, z, out = refs[:6]
    *local, sems = refs[6:]
    copies = [pltpu.make_async_copy(a, b, sems.at[n]) for n, (a, b) in enumerate(zip(small, local))]
    big = pltpu.make_async_copy(z, out.at[pl.ds(0, 1024)], sems.at[4])
    for copy in copies + [big]:
        copy.start()
    for copy in copies:
        copy.wait()
    z_cols, z_count, h_cols, h_count = local
    row = lax.axis_index("rows")
    slot = lax.axis_index("x") * 2 + lax.axis_index("core")
    turn = (row % 2) * 2 * HB
    for line, (cols, count) in enumerate(((z_cols, z_count), (h_cols, h_count))):
        for i in range(HB):
            place = cols[i] - (row * HB - HB)
            place = jnp.where(place < HB, place + turn, jnp.where(place < 2 * HB, place, place - turn))
            place = jnp.where(slot < count[i], place, -1).astype(jnp.float32)
            out[pl.ds(1024 + line * HB + i, 1), :] = jnp.full((1, 256), place, jnp.float32)
    big.wait()


def pack_kernel(own, below, above, out):
    for t in range(2):
        for j in range(HB):
            total = (
                own[j, :, pl.ds(128 * t, 128)]
                + below[j, :, pl.ds(128 * t, 128)]
                + above[j, :, pl.ds(128 * t, 128)]
            )
            for u in range(4):
                shift = (32 * (j - u)) % 128
                turned = total if shift == 0 else pltpu.roll(total, shift, 1)
                out[4 * t + u, :, pl.ds(32 * j, 32)] = turned[:, 32 * j : 32 * j + 32]


def final_kernel(parts, out):
    halves = []
    for q in range(2):
        halves.append((parts[q] + parts[2 + q]) + (parts[4 + q] + parts[6 + q]))
    total = jnp.concatenate(halves + halves, axis=0)
    out[...] = jnp.transpose(total)[:, :64].reshape(out.shape)


def call(kernel, out_shape, count, flops, size):
    return pl.pallas_call(
        kernel,
        out_shape=out_shape,
        in_specs=[VMEM] * count,
        out_specs=jax.tree.map(lambda _: VMEM, out_shape),
        cost_estimate=pl.CostEstimate(flops=flops, bytes_accessed=size, transcendentals=0),
        compiler_params=pltpu.CompilerParams(vmem_limit_bytes=8 << 20),
    )


def f32(*shape):
    return jax.ShapeDtypeStruct(shape, jnp.float32)


def neighbours(first, second):
    count = lax.axis_size("rows")
    results = []
    for field, offset in ((first, 1), (second, 0)):
        pairs = [(i, i + 1) for i in range(offset, count - 1, 2)]
        results.append(lax.ppermute(field, "rows", pairs + [(b, a) for a, b in pairs]))
    return results


def steps(z_blocks, z_cols, z_count, h_blocks, h_cols, h_count, panel):
    q = lax.axis_index("core")
    z = z_blocks.reshape(1024, 256)
    h = h_blocks.reshape(1024, 256)
    hbm = pl.BlockSpec(memory_space=pltpu.HBM)
    operands = (z_cols.reshape(HB), z_count, h_cols.reshape(HB), h_count, z)
    mine = pl.pallas_call(
        stage_kernel,
        out_shape=f32(1032, 256),
        in_specs=[hbm] * 5,
        out_specs=VMEM,
        scratch_shapes=[pltpu.SMEM((HB,), jnp.int32)] * 4 + [pltpu.SemaphoreType.DMA((5,))],
        compiler_params=pltpu.CompilerParams(vmem_limit_bytes=4 << 20),
        name="stage",
    )(*(pltpu.with_memory_space_constraint(a, pltpu.HBM) for a in operands))
    mine, panel = lax.optimization_barrier((mine, panel))

    swap = [(0, 1), (1, 0)]
    x = lax.dynamic_slice_in_dim(jnp.swapaxes(panel, 1, 2), q * 32, 32, axis=1)
    x_first, x_second = neighbours(x, x)
    theirs = lax.ppermute(mine, "core", swap)
    h_theirs = lax.ppermute(h, "core", swap)

    def forward(line, first, own, second, blocks, other):
        body = lambda *refs: forward_kernel(line, *refs)
        parts = call(body, f32(4, HB, 32, 256), 7, 1 << 28, 1 << 22)(first, own, second, blocks, other, mine, theirs)
        return lax.all_to_all(parts, "x", 0, 0, tiled=True)

    mid = forward(0, x_first, x, x_second, mine, theirs)
    mid = call(fold_kernel, f32(HB, 32, 256), 1, 1 << 18, 1 << 19)(mid)
    mid_first, mid_second = neighbours(mid, mid)
    side = forward(4, mid_first, mid, mid_second, h, h_theirs)
    shape = f32(HB, 32, 256)
    first, own, second = call(backward_kernel, (shape, shape, shape), 5, 1 << 28, 1 << 22)(
        side, mine, theirs, mine, theirs
    )
    first, second = neighbours(first, second)
    packed = call(pack_kernel, f32(8, 32, 128), 3, 1 << 20, 1 << 20)(own, first, second)
    arrived = lax.all_to_all(packed, ("x", "core"), 0, 0, tiled=True)
    return call(final_kernel, f32(HB, 32, 64), 1, 1 << 20, 1 << 18)(arrived)


def solution(mesh):
    grid = Mesh(mesh.devices.reshape(mesh.shape["rows"], 4, 2), ("rows", "x", "core"))
    cols = ("x", "core")
    return jax.shard_map(
        steps,
        mesh=grid,
        in_specs=(
            P("rows", cols, None, None),
            P("rows", cols),
            P("rows"),
            P("rows", cols, None, None),
            P("rows", cols),
            P("rows"),
            P("rows", None, None),
        ),
        out_specs=P("rows", cols, None),
        check_vma=False,
    )
```

```python
import jax
import jax.numpy as jnp
from jax import lax
from jax.experimental import pallas as pl
from jax.experimental.pallas import tpu as pltpu
from jax.sharding import Mesh, PartitionSpec as P


HB = 4
VMEM = pl.BlockSpec(memory_space=pltpu.VMEM)


def split(x):
    high = x.astype(jnp.bfloat16)
    low = (x - high.astype(jnp.float32)).astype(jnp.bfloat16)
    return high, low


def product(x, block, dims):
    m = x.shape[0]
    xh, xl = split(x)
    bh, bl = split(block)
    dot = lambda a, b: lax.dot_general(a, b, (dims, ((), ())), preferred_element_type=jnp.float32)
    both = dot(jnp.concatenate([xh, xl], axis=0), bh)
    return both[:m] + (both[m:] + dot(xh, bl))


def pick(fields, index):
    picked = jnp.zeros(fields[0].shape, jnp.float32)
    for w, field in enumerate(fields):
        picked = jnp.where(index == w, field, picked)
    return picked


def forward_kernel(row, low, own, high, mine, theirs, index_mine, index_theirs, out):
    n = own.shape[1]
    fields = [ref[j] for ref in (low, own, high) for j in range(HB)]
    turned = fields[2 * HB :] + fields[HB : 2 * HB] + fields[:HB]
    for i in range(HB):
        total = None
        for blocks, index, window in ((mine, index_mine, fields), (theirs, index_theirs, turned)):
            where = jnp.broadcast_to(index[pl.ds(index.shape[0] - 8 + row + i, 1), :], (n, 256))
            part = product(pick(window, where), blocks[pl.ds(i * 256, 256), :], ((1,), (1,)))
            total = part if total is None else total + part
        for x in range(out.shape[0]):
            out[x, i] = total


def backward_kernel(parts, mine, theirs, index_mine, index_theirs, low, own, high):
    n = own.shape[1]
    outs = [(ref, j) for ref in (low, own, high) for j in range(HB)]
    turned = outs[2 * HB :] + outs[HB : 2 * HB] + outs[:HB]
    for ref, j in outs:
        ref[j] = jnp.zeros((n, 256), jnp.float32)
    for i in range(HB):
        side = (parts[0, i] + parts[1, i]) + (parts[2, i] + parts[3, i])
        for blocks, index, window in ((mine, index_mine, outs), (theirs, index_theirs, turned)):
            where = jnp.broadcast_to(index[pl.ds(index.shape[0] - 8 + i, 1), :], (n, 256))
            term = product(side, blocks[pl.ds(i * 256, 256), :], ((1,), (0,)))
            for w, (ref, j) in enumerate(window):
                ref[j] = ref[j] + jnp.where(where == w, term, 0.0)


def fold_kernel(parts, out):
    out[...] = (parts[0] + parts[1]) + (parts[2] + parts[3])


def stage_kernel(*refs):
    *small, z, out = refs[:6]
    *local, sems = refs[6:]
    copies = [pltpu.make_async_copy(a, b, sems.at[n]) for n, (a, b) in enumerate(zip(small, local))]
    big = pltpu.make_async_copy(z, out.at[pl.ds(0, 1024)], sems.at[4])
    for copy in copies + [big]:
        copy.start()
    for copy in copies:
        copy.wait()
    z_cols, z_count, h_cols, h_count = local
    row = lax.axis_index("rows")
    slot = lax.axis_index("x") * 2 + lax.axis_index("core")
    turn = ((row + lax.axis_index("core")) % 2) * 2 * HB
    for line, (cols, count) in enumerate(((z_cols, z_count), (h_cols, h_count))):
        for i in range(HB):
            place = cols[i] - (row * HB - HB)
            place = jnp.where(place < HB, place + turn, jnp.where(place < 2 * HB, place, place - turn))
            place = jnp.where(slot < count[i], place, -1).astype(jnp.float32)
            out[pl.ds(1024 + line * HB + i, 1), :] = jnp.full((1, 256), place, jnp.float32)
    big.wait()


def pack_kernel(own, below, above, out):
    for t in range(2):
        for j in range(HB):
            total = (
                own[j, :, pl.ds(128 * t, 128)]
                + below[j, :, pl.ds(128 * t, 128)]
                + above[j, :, pl.ds(128 * t, 128)]
            )
            for u in range(4):
                shift = (32 * (j - u)) % 128
                turned = total if shift == 0 else pltpu.roll(total, shift, 1)
                out[4 * t + u, :, pl.ds(32 * j, 32)] = turned[:, 32 * j : 32 * j + 32]


def final_kernel(parts, out):
    halves = []
    for q in range(2):
        halves.append((parts[q] + parts[2 + q]) + (parts[4 + q] + parts[6 + q]))
    total = jnp.concatenate(halves + halves, axis=0)
    out[...] = jnp.transpose(total)[:, :64].reshape(out.shape)


def call(kernel, out_shape, count, flops, size):
    return pl.pallas_call(
        kernel,
        out_shape=out_shape,
        in_specs=[VMEM] * count,
        out_specs=jax.tree.map(lambda _: VMEM, out_shape),
        cost_estimate=pl.CostEstimate(flops=flops, bytes_accessed=size, transcendentals=0),
        compiler_params=pltpu.CompilerParams(vmem_limit_bytes=8 << 20),
    )


def f32(*shape):
    return jax.ShapeDtypeStruct(shape, jnp.float32)


def neighbours(first, second):
    count = lax.axis_size("rows")
    results = []
    for field, step in ((first, 0), (second, 1)):
        pairs = []
        for core in range(2):
            pairs += [(2 * i + core, 2 * i + 2 + core) for i in range((core + step + 1) % 2, count - 1, 2)]
        results.append(lax.ppermute(field, ("rows", "core"), pairs + [(b, a) for a, b in pairs]))
    return results


def steps(z_blocks, z_cols, z_count, h_blocks, h_cols, h_count, panel):
    q = lax.axis_index("core")
    z = z_blocks.reshape(1024, 256)
    h = h_blocks.reshape(1024, 256)
    hbm = pl.BlockSpec(memory_space=pltpu.HBM)
    operands = (z_cols.reshape(HB), z_count, h_cols.reshape(HB), h_count, z)
    mine = pl.pallas_call(
        stage_kernel,
        out_shape=f32(1032, 256),
        in_specs=[hbm] * 5,
        out_specs=VMEM,
        scratch_shapes=[pltpu.SMEM((HB,), jnp.int32)] * 4 + [pltpu.SemaphoreType.DMA((5,))],
        compiler_params=pltpu.CompilerParams(vmem_limit_bytes=4 << 20),
        name="stage",
    )(*(pltpu.with_memory_space_constraint(a, pltpu.HBM) for a in operands))
    mine, panel = lax.optimization_barrier((mine, panel))

    swap = [(0, 1), (1, 0)]
    x = lax.dynamic_slice_in_dim(jnp.swapaxes(panel, 1, 2), q * 32, 32, axis=1)
    x_first, x_second = neighbours(x, x)
    theirs = lax.ppermute(mine, "core", swap)
    h_theirs = lax.ppermute(h, "core", swap)

    def forward(line, first, own, second, blocks, other):
        body = lambda *refs: forward_kernel(line, *refs)
        parts = call(body, f32(4, HB, 32, 256), 7, 1 << 28, 1 << 22)(first, own, second, blocks, other, mine, theirs)
        return lax.all_to_all(parts, "x", 0, 0, tiled=True)

    mid = forward(0, x_first, x, x_second, mine, theirs)
    mid = call(fold_kernel, f32(HB, 32, 256), 1, 1 << 18, 1 << 19)(mid)
    mid_first, mid_second = neighbours(mid, mid)
    side = forward(4, mid_first, mid, mid_second, h, h_theirs)
    shape = f32(HB, 32, 256)
    first, own, second = call(backward_kernel, (shape, shape, shape), 5, 1 << 28, 1 << 22)(
        side, mine, theirs, mine, theirs
    )
    first, second = neighbours(first, second)
    packed = call(pack_kernel, f32(8, 32, 128), 3, 1 << 20, 1 << 20)(own, first, second)
    arrived = lax.all_to_all(packed, ("x", "core"), 0, 0, tiled=True)
    return call(final_kernel, f32(HB, 32, 64), 1, 1 << 20, 1 << 18)(arrived)


def solution(mesh):
    grid = Mesh(mesh.devices.reshape(mesh.shape["rows"], 4, 2), ("rows", "x", "core"))
    cols = ("x", "core")
    return jax.shard_map(
        steps,
        mesh=grid,
        in_specs=(
            P("rows", cols, None, None),
            P("rows", cols),
            P("rows"),
            P("rows", cols, None, None),
            P("rows", cols),
            P("rows"),
            P("rows", None, None),
        ),
        out_specs=P("rows", cols, None),
        check_vma=False,
    )
```

```python
import jax
import jax.numpy as jnp
from jax import lax
from jax.experimental import pallas as pl
from jax.experimental.pallas import tpu as pltpu
from jax.sharding import Mesh, PartitionSpec as P


HB = 4
VMEM = pl.BlockSpec(memory_space=pltpu.VMEM)


def split(x):
    high = x.astype(jnp.bfloat16)
    low = (x - high.astype(jnp.float32)).astype(jnp.bfloat16)
    return high, low


def product(x, high, low, dims):
    m = x.shape[0]
    xh, xl = split(x)
    dot = lambda a, b: lax.dot_general(a, b, (dims, ((), ())), preferred_element_type=jnp.float32)
    both = dot(jnp.concatenate([xh, xl], axis=0), high)
    return both[:m] + (both[m:] + dot(xh, low))


def index_tile(index, line):
    return jnp.broadcast_to(index[pl.ds(1024 + line, 1), :], (8, 256))[None]


def swapped(thirds):
    return thirds[2 * HB :] + thirds[HB : 2 * HB] + thirds[:HB]


def pick(fields, index):
    picked = jnp.zeros(fields[0].shape, jnp.float32)
    for w, field in enumerate(fields):
        picked = jnp.where(index == w, field, picked)
    return picked


def split_kernel(*refs):
    count = len(refs) // 3
    for block, high, low in zip(refs[:count], refs[count::2], refs[count + 1 :: 2]):
        for i in range(HB):
            rows = pl.ds(i * 256, 256)
            high[rows, :], low[rows, :] = split(block[rows, :])


def forward_kernel(line, parts, first, own, second, index_mine, index_theirs, *refs):
    *blocks, out = refs
    n = own.shape[1]
    fields = [ref[j].reshape(n // 8, 8, 256) for ref in (first, own, second) for j in range(HB)]
    for i in range(HB):
        rows = pl.ds(i * 256, 256)
        total = None
        for s, (index, window) in enumerate(((index_mine, fields), (index_theirs, swapped(fields)))):
            high, low = (blocks[2 * s][rows, :], blocks[2 * s + 1][rows, :]) if parts else split(blocks[s][rows, :])
            part = product(pick(window, index_tile(index, line + i)).reshape(n, 256), high, low, ((1,), (1,)))
            total = part if total is None else total + part
        for x in range(out.shape[0]):
            out[x, i] = total


def backward_kernel(parts, index_mine, index_theirs, mine_high, mine_low, theirs_high, theirs_low, first, own, second):
    n = own.shape[1]
    mine, theirs = [], []
    for i in range(HB):
        rows = pl.ds(i * 256, 256)
        side = (parts[0, i] + parts[1, i]) + (parts[2, i] + parts[3, i])
        for terms, index, high, low in (
            (mine, index_mine, mine_high, mine_low),
            (theirs, index_theirs, theirs_high, theirs_low),
        ):
            term = product(side, high[rows, :], low[rows, :], ((1,), (0,)))
            terms.append((index_tile(index, i), term.reshape(n // 8, 8, 256)))
    outs = [(ref, j) for ref in (first, own, second) for j in range(HB)]
    order = swapped(list(range(3 * HB)))
    for w, (ref, j) in enumerate(outs):
        total = jnp.zeros((n // 8, 8, 256), jnp.float32)
        for terms, place in ((mine, w), (theirs, order[w])):
            for index, term in terms:
                total = total + jnp.where(index == place, term, 0.0)
        ref[j] = total.reshape(n, 256)


def fold_kernel(parts, out):
    out[...] = (parts[0] + parts[1]) + (parts[2] + parts[3])


def stage_kernel(*refs):
    *small, z, out = refs[:6]
    *local, sems = refs[6:]
    copies = [pltpu.make_async_copy(a, b, sems.at[n]) for n, (a, b) in enumerate(zip(small, local))]
    big = pltpu.make_async_copy(z, out.at[pl.ds(0, 1024)], sems.at[4])
    for copy in copies + [big]:
        copy.start()
    for copy in copies:
        copy.wait()
    z_cols, z_count, h_cols, h_count = local
    row = lax.axis_index("rows")
    slot = lax.axis_index("x") * 2 + lax.axis_index("core")
    turn = ((row + lax.axis_index("core")) % 2) * 2 * HB
    for line, (cols, count) in enumerate(((z_cols, z_count), (h_cols, h_count))):
        for i in range(HB):
            place = cols[i] - (row * HB - HB)
            place = jnp.where(place < HB, place + turn, jnp.where(place < 2 * HB, place, place - turn))
            place = jnp.where(slot < count[i], place, -1).astype(jnp.float32)
            out[pl.ds(1024 + line * HB + i, 1), :] = jnp.full((1, 256), place, jnp.float32)
    big.wait()


def pack_kernel(own, below, above, out):
    for t in range(2):
        for j in range(HB):
            total = (
                own[j, :, pl.ds(128 * t, 128)]
                + below[j, :, pl.ds(128 * t, 128)]
                + above[j, :, pl.ds(128 * t, 128)]
            )
            for u in range(4):
                shift = (32 * (j - u)) % 128
                turned = total if shift == 0 else pltpu.roll(total, shift, 1)
                out[4 * t + u, :, pl.ds(32 * j, 32)] = turned[:, 32 * j : 32 * j + 32]


def final_kernel(parts, out):
    halves = []
    for q in range(2):
        halves.append((parts[q] + parts[2 + q]) + (parts[4 + q] + parts[6 + q]))
    total = jnp.concatenate(halves + halves, axis=0)
    out[...] = jnp.transpose(total)[:, :64].reshape(out.shape)


def call(kernel, out_shape, count, flops, size):
    return pl.pallas_call(
        kernel,
        out_shape=out_shape,
        in_specs=[VMEM] * count,
        out_specs=jax.tree.map(lambda _: VMEM, out_shape),
        cost_estimate=pl.CostEstimate(flops=flops, bytes_accessed=size, transcendentals=0),
        compiler_params=pltpu.CompilerParams(vmem_limit_bytes=8 << 20),
    )


def f32(*shape):
    return jax.ShapeDtypeStruct(shape, jnp.float32)


def neighbours(first, second):
    count = lax.axis_size("rows")
    results = []
    for field, step in ((first, 0), (second, 1)):
        pairs = []
        for core in range(2):
            pairs += [(2 * i + core, 2 * i + 2 + core) for i in range((core + step + 1) % 2, count - 1, 2)]
        results.append(lax.ppermute(field, ("rows", "core"), pairs + [(b, a) for a, b in pairs]))
    return results


def steps(z_blocks, z_cols, z_count, h_blocks, h_cols, h_count, panel):
    q = lax.axis_index("core")
    z = z_blocks.reshape(1024, 256)
    h = h_blocks.reshape(1024, 256)
    hbm = pl.BlockSpec(memory_space=pltpu.HBM)
    operands = (z_cols.reshape(HB), z_count, h_cols.reshape(HB), h_count, z)
    mine = pl.pallas_call(
        stage_kernel,
        out_shape=f32(1032, 256),
        in_specs=[hbm] * 5,
        out_specs=VMEM,
        scratch_shapes=[pltpu.SMEM((HB,), jnp.int32)] * 4 + [pltpu.SemaphoreType.DMA((5,))],
        compiler_params=pltpu.CompilerParams(vmem_limit_bytes=4 << 20),
        name="stage",
    )(*(pltpu.with_memory_space_constraint(a, pltpu.HBM) for a in operands))
    mine, panel, h = lax.optimization_barrier((mine, panel, h))

    swap = [(0, 1), (1, 0)]
    x = lax.dynamic_slice_in_dim(jnp.swapaxes(panel, 1, 2), q * 32, 32, axis=1)
    x_first, x_second = neighbours(x, x)
    theirs = lax.ppermute(mine, "core", swap)
    h_theirs = lax.ppermute(h, "core", swap)

    def forward(line, first, own, second, blocks):
        body = lambda *refs: forward_kernel(line, len(blocks) == 4, *refs)
        operands = (first, own, second, mine, theirs, *blocks)
        parts = call(body, f32(4, HB, 32, 256), len(operands), 1 << 28, 1 << 22)(*operands)
        return lax.all_to_all(parts, "x", 0, 0, tiled=True)

    mid = forward(0, x_first, x, x_second, (mine, theirs))
    mid = call(fold_kernel, f32(HB, 32, 256), 1, 1 << 18, 1 << 19)(mid)
    mid_first, mid_second = neighbours(mid, mid)
    half = jax.ShapeDtypeStruct((1024, 256), jnp.bfloat16)
    parts = call(split_kernel, (half,) * 8, 4, 1 << 20, 1 << 23)(h, h_theirs, mine, theirs)
    side = forward(4, mid_first, mid, mid_second, parts[:4])
    shape = f32(HB, 32, 256)
    first, own, second = call(backward_kernel, (shape, shape, shape), 7, 1 << 28, 1 << 22)(
        side, mine, theirs, *parts[4:]
    )
    first, second = neighbours(first, second)
    packed = call(pack_kernel, f32(8, 32, 128), 3, 1 << 20, 1 << 20)(own, first, second)
    arrived = lax.all_to_all(packed, ("x", "core"), 0, 0, tiled=True)
    return call(final_kernel, f32(HB, 32, 64), 1, 1 << 20, 1 << 18)(arrived)


def solution(mesh):
    grid = Mesh(mesh.devices.reshape(mesh.shape["rows"], 4, 2), ("rows", "x", "core"))
    cols = ("x", "core")
    return jax.shard_map(
        steps,
        mesh=grid,
        in_specs=(
            P("rows", cols, None, None),
            P("rows", cols),
            P("rows"),
            P("rows", cols, None, None),
            P("rows", cols),
            P("rows"),
            P("rows", None, None),
        ),
        out_specs=P("rows", cols, None),
        check_vma=False,
    )
```

```python
import jax
import jax.numpy as jnp
from jax import lax
from jax.experimental import pallas as pl
from jax.experimental.pallas import tpu as pltpu
from jax.sharding import Mesh, PartitionSpec as P


HB = 4
VMEM = pl.BlockSpec(memory_space=pltpu.VMEM)


def split(x):
    high = x.astype(jnp.bfloat16)
    low = (x - high.astype(jnp.float32)).astype(jnp.bfloat16)
    return high, low


def product(x, high, low, dims):
    m = x.shape[0]
    xh, xl = split(x)
    dot = lambda a, b: lax.dot_general(a, b, (dims, ((), ())), preferred_element_type=jnp.float32)
    both = dot(jnp.concatenate([xh, xl], axis=0), high)
    return both[:m] + (both[m:] + dot(xh, low))


def index_tile(index, line):
    return jnp.broadcast_to(index[pl.ds(1024 + line, 1), :], (8, 256))[None]


def swapped(thirds):
    return thirds[2 * HB :] + thirds[HB : 2 * HB] + thirds[:HB]


def pick(fields, index):
    picked = jnp.zeros(fields[0].shape, jnp.float32)
    for w, field in enumerate(fields):
        picked = jnp.where(index == w, field, picked)
    return picked


def split_kernel(*refs):
    count = len(refs) // 3
    for block, high, low in zip(refs[:count], refs[count::2], refs[count + 1 :: 2]):
        for i in range(HB):
            rows = pl.ds(i * 256, 256)
            high[rows, :], low[rows, :] = split(block[rows, :])


def forward_kernel(line, parts, first, own, second, index_mine, index_theirs, *refs):
    *blocks, out = refs
    n = own.shape[1]
    fields = [ref[j].reshape(n // 8, 8, 256) for ref in (first, own, second) for j in range(HB)]
    for i in range(HB):
        rows = pl.ds(i * 256, 256)
        total = None
        for s, (index, window) in enumerate(((index_mine, fields), (index_theirs, swapped(fields)))):
            high, low = (blocks[2 * s][rows, :], blocks[2 * s + 1][rows, :]) if parts else split(blocks[s][rows, :])
            part = product(pick(window, index_tile(index, line + i)).reshape(n, 256), high, low, ((1,), (1,)))
            total = part if total is None else total + part
        for x in range(out.shape[0]):
            out[x, i] = total


def backward_kernel(parts, index_mine, index_theirs, mine_high, mine_low, theirs_high, theirs_low, first, own, second):
    n = own.shape[1]
    mine, theirs = [], []
    for i in range(HB):
        rows = pl.ds(i * 256, 256)
        side = (parts[0, i] + parts[1, i]) + (parts[2, i] + parts[3, i])
        for terms, index, high, low in (
            (mine, index_mine, mine_high, mine_low),
            (theirs, index_theirs, theirs_high, theirs_low),
        ):
            term = product(side, high[rows, :], low[rows, :], ((1,), (0,)))
            terms.append((index_tile(index, i), term.reshape(n // 8, 8, 256)))
    outs = [(ref, j) for ref in (first, own, second) for j in range(HB)]
    order = swapped(list(range(3 * HB)))
    for w, (ref, j) in enumerate(outs):
        total = jnp.zeros((n // 8, 8, 256), jnp.float32)
        for terms, place in ((mine, w), (theirs, order[w])):
            for index, term in terms:
                total = total + jnp.where(index == place, term, 0.0)
        ref[j] = total.reshape(n, 256)


def fold_kernel(own, second, first, third, out):
    out[...] = (own[...] + first[...]) + (second[...] + third[...])


def stage_kernel(*refs):
    *small, z, out = refs[:6]
    *local, sems = refs[6:]
    copies = [pltpu.make_async_copy(a, b, sems.at[n]) for n, (a, b) in enumerate(zip(small, local))]
    big = pltpu.make_async_copy(z, out.at[pl.ds(0, 1024)], sems.at[4])
    for copy in copies + [big]:
        copy.start()
    for copy in copies:
        copy.wait()
    z_cols, z_count, h_cols, h_count = local
    row = lax.axis_index("rows")
    slot = lax.axis_index("x") * 2 + lax.axis_index("core")
    turn = ((row + lax.axis_index("core")) % 2) * 2 * HB
    for line, (cols, count) in enumerate(((z_cols, z_count), (h_cols, h_count))):
        for i in range(HB):
            place = cols[i] - (row * HB - HB)
            place = jnp.where(place < HB, place + turn, jnp.where(place < 2 * HB, place, place - turn))
            place = jnp.where(slot < count[i], place, -1).astype(jnp.float32)
            out[pl.ds(1024 + line * HB + i, 1), :] = jnp.full((1, 256), place, jnp.float32)
    big.wait()


def pack_kernel(own, below, above, out):
    for t in range(2):
        for j in range(HB):
            total = (
                own[j, :, pl.ds(128 * t, 128)]
                + below[j, :, pl.ds(128 * t, 128)]
                + above[j, :, pl.ds(128 * t, 128)]
            )
            for u in range(4):
                shift = (32 * (j - u)) % 128
                turned = total if shift == 0 else pltpu.roll(total, shift, 1)
                out[4 * t + u, :, pl.ds(32 * j, 32)] = turned[:, 32 * j : 32 * j + 32]


def final_kernel(parts, out):
    halves = []
    for q in range(2):
        halves.append((parts[q] + parts[2 + q]) + (parts[4 + q] + parts[6 + q]))
    total = jnp.concatenate(halves + halves, axis=0)
    out[...] = jnp.transpose(total)[:, :64].reshape(out.shape)


def call(kernel, out_shape, count, flops, size):
    return pl.pallas_call(
        kernel,
        out_shape=out_shape,
        in_specs=[VMEM] * count,
        out_specs=jax.tree.map(lambda _: VMEM, out_shape),
        cost_estimate=pl.CostEstimate(flops=flops, bytes_accessed=size, transcendentals=0),
        compiler_params=pltpu.CompilerParams(vmem_limit_bytes=8 << 20),
    )


def f32(*shape):
    return jax.ShapeDtypeStruct(shape, jnp.float32)


def neighbours(first, second):
    count = lax.axis_size("rows")
    results = []
    for field, step in ((first, 0), (second, 1)):
        pairs = []
        for core in range(2):
            pairs += [(2 * i + core, 2 * i + 2 + core) for i in range((core + step + 1) % 2, count - 1, 2)]
        results.append(lax.ppermute(field, ("rows", "core"), pairs + [(b, a) for a, b in pairs]))
    return results


def steps(z_blocks, z_cols, z_count, h_blocks, h_cols, h_count, panel):
    q = lax.axis_index("core")
    z = z_blocks.reshape(1024, 256)
    h = h_blocks.reshape(1024, 256)
    hbm = pl.BlockSpec(memory_space=pltpu.HBM)
    operands = (z_cols.reshape(HB), z_count, h_cols.reshape(HB), h_count, z)
    mine = pl.pallas_call(
        stage_kernel,
        out_shape=f32(1032, 256),
        in_specs=[hbm] * 5,
        out_specs=VMEM,
        scratch_shapes=[pltpu.SMEM((HB,), jnp.int32)] * 4 + [pltpu.SemaphoreType.DMA((5,))],
        compiler_params=pltpu.CompilerParams(vmem_limit_bytes=4 << 20),
        name="stage",
    )(*(pltpu.with_memory_space_constraint(a, pltpu.HBM) for a in operands))
    mine, panel, h = lax.optimization_barrier((mine, panel, h))

    swap = [(0, 1), (1, 0)]
    x = lax.dynamic_slice_in_dim(jnp.swapaxes(panel, 1, 2), q * 32, 32, axis=1)
    x_first, x_second = neighbours(x, x)
    theirs = lax.ppermute(mine, "core", swap)
    h_theirs = lax.ppermute(h, "core", swap)

    def forward(line, first, own, second, blocks, copies):
        body = lambda *refs: forward_kernel(line, len(blocks) == 4, *refs)
        operands = (first, own, second, mine, theirs, *blocks)
        return call(body, f32(copies, HB, 32, 256), len(operands), 1 << 28, 1 << 22)(*operands)

    mids = [forward(0, x_first, x, x_second, (mine, theirs), 1).reshape(HB, 32, 256)]
    for step in (2, 1, 3):
        mids.append(lax.ppermute(mids[0], "x", [(i, i ^ step) for i in range(4)]))
    mid = call(fold_kernel, f32(HB, 32, 256), 4, 1 << 18, 1 << 19)(*mids)
    mid_first, mid_second = neighbours(mid, mid)
    half = jax.ShapeDtypeStruct((1024, 256), jnp.bfloat16)
    parts = call(split_kernel, (half,) * 8, 4, 1 << 20, 1 << 23)(h, h_theirs, mine, theirs)
    side = forward(4, mid_first, mid, mid_second, parts[:4], 4)
    side = lax.all_to_all(side, "x", 0, 0, tiled=True)
    shape = f32(HB, 32, 256)
    first, own, second = call(backward_kernel, (shape, shape, shape), 7, 1 << 28, 1 << 22)(
        side, mine, theirs, *parts[4:]
    )
    first, second = neighbours(first, second)
    packed = call(pack_kernel, f32(8, 32, 128), 3, 1 << 20, 1 << 20)(own, first, second)
    arrived = lax.all_to_all(packed, ("x", "core"), 0, 0, tiled=True)
    return call(final_kernel, f32(HB, 32, 64), 1, 1 << 20, 1 << 18)(arrived)


def solution(mesh):
    grid = Mesh(mesh.devices.reshape(mesh.shape["rows"], 4, 2), ("rows", "x", "core"))
    cols = ("x", "core")
    return jax.shard_map(
        steps,
        mesh=grid,
        in_specs=(
            P("rows", cols, None, None),
            P("rows", cols),
            P("rows"),
            P("rows", cols, None, None),
            P("rows", cols),
            P("rows"),
            P("rows", None, None),
        ),
        out_specs=P("rows", cols, None),
        check_vma=False,
    )
```

```python
import jax
import jax.numpy as jnp
from jax import lax
from jax.experimental import pallas as pl
from jax.experimental.pallas import tpu as pltpu
from jax.sharding import Mesh, PartitionSpec as P


HB = 4
VMEM = pl.BlockSpec(memory_space=pltpu.VMEM)


def split(x):
    high = x.astype(jnp.bfloat16)
    low = (x - high.astype(jnp.float32)).astype(jnp.bfloat16)
    return high, low


def product(x, high, low, dims):
    m = x.shape[0]
    xh, xl = split(x)
    dot = lambda a, b: lax.dot_general(a, b, (dims, ((), ())), preferred_element_type=jnp.float32)
    both = dot(jnp.concatenate([xh, xl], axis=0), high)
    return both[:m] + (both[m:] + dot(xh, low))


def index_tile(index, line):
    return jnp.broadcast_to(index[pl.ds(1024 + line, 1), :], (8, 256))[None]


def swapped(thirds):
    return thirds[2 * HB :] + thirds[HB : 2 * HB] + thirds[:HB]


def pick(fields, index):
    picked = jnp.zeros(fields[0].shape, jnp.float32)
    for w, field in enumerate(fields):
        picked = jnp.where(index == w, field, picked)
    return picked


def split_kernel(*refs):
    count = len(refs) // 3
    for k, (block, high, low) in enumerate(zip(refs[:count], refs[count::2], refs[count + 1 :: 2])):
        for i in range(HB):
            rows = pl.ds(i * 256, 256)
            whole = block[rows, :]
            high[rows, :], low[rows, :] = split(jnp.transpose(whole) if k < 2 else whole)


def forward_kernel(line, parts, first, own, second, index_mine, index_theirs, *refs):
    *blocks, out = refs
    n = own.shape[1]
    fields = [ref[j].reshape(n // 8, 8, 256) for ref in (first, own, second) for j in range(HB)]
    for i in range(HB):
        rows = pl.ds(i * 256, 256)
        total = None
        for s, (index, window) in enumerate(((index_mine, fields), (index_theirs, swapped(fields)))):
            high, low = (blocks[2 * s][rows, :], blocks[2 * s + 1][rows, :]) if parts else split(blocks[s][rows, :])
            picked = pick(window, index_tile(index, line + i)).reshape(n, 256)
            part = product(picked, high, low, ((1,), (0,) if parts else (1,)))
            total = part if total is None else total + part
        for x in range(out.shape[0]):
            out[x, i] = total


def backward_kernel(parts, index_mine, index_theirs, mine_high, mine_low, theirs_high, theirs_low, first, own, second):
    n = own.shape[1]
    mine, theirs = [], []
    for i in range(HB):
        rows = pl.ds(i * 256, 256)
        side = (parts[0, i] + parts[1, i]) + (parts[2, i] + parts[3, i])
        for terms, index, high, low in (
            (mine, index_mine, mine_high, mine_low),
            (theirs, index_theirs, theirs_high, theirs_low),
        ):
            term = product(side, high[rows, :], low[rows, :], ((1,), (0,)))
            terms.append((index_tile(index, i), term.reshape(n // 8, 8, 256)))
    outs = [(ref, j) for ref in (first, own, second) for j in range(HB)]
    order = swapped(list(range(3 * HB)))
    for w, (ref, j) in enumerate(outs):
        total = jnp.zeros((n // 8, 8, 256), jnp.float32)
        for terms, place in ((mine, w), (theirs, order[w])):
            for index, term in terms:
                total = total + jnp.where(index == place, term, 0.0)
        ref[j] = total.reshape(n, 256)


def fold_kernel(parts, out):
    out[...] = (parts[0] + parts[1]) + (parts[2] + parts[3])


def stage_kernel(*refs):
    *small, z, out = refs[:6]
    *local, sems = refs[6:]
    copies = [pltpu.make_async_copy(a, b, sems.at[n]) for n, (a, b) in enumerate(zip(small, local))]
    big = pltpu.make_async_copy(z, out.at[pl.ds(0, 1024)], sems.at[4])
    for copy in copies + [big]:
        copy.start()
    for copy in copies:
        copy.wait()
    z_cols, z_count, h_cols, h_count = local
    row = lax.axis_index("rows")
    slot = lax.axis_index("x") * 2 + lax.axis_index("core")
    turn = ((row + lax.axis_index("core")) % 2) * 2 * HB
    for line, (cols, count) in enumerate(((z_cols, z_count), (h_cols, h_count))):
        for i in range(HB):
            place = cols[i] - (row * HB - HB)
            place = jnp.where(place < HB, place + turn, jnp.where(place < 2 * HB, place, place - turn))
            place = jnp.where(slot < count[i], place, -1).astype(jnp.float32)
            out[pl.ds(1024 + line * HB + i, 1), :] = jnp.full((1, 256), place, jnp.float32)
    big.wait()


def pack_kernel(own, below, above, out):
    for t in range(2):
        for j in range(HB):
            total = (
                own[j, :, pl.ds(128 * t, 128)]
                + below[j, :, pl.ds(128 * t, 128)]
                + above[j, :, pl.ds(128 * t, 128)]
            )
            for u in range(4):
                shift = (32 * (j - u)) % 128
                turned = total if shift == 0 else pltpu.roll(total, shift, 1)
                out[4 * t + u, :, pl.ds(32 * j, 32)] = turned[:, 32 * j : 32 * j + 32]


def final_kernel(parts, out):
    halves = []
    for q in range(2):
        halves.append((parts[q] + parts[2 + q]) + (parts[4 + q] + parts[6 + q]))
    total = jnp.concatenate(halves + halves, axis=0)
    out[...] = jnp.transpose(total)[:, :64].reshape(out.shape)


def call(kernel, out_shape, count, flops, size):
    return pl.pallas_call(
        kernel,
        out_shape=out_shape,
        in_specs=[VMEM] * count,
        out_specs=jax.tree.map(lambda _: VMEM, out_shape),
        cost_estimate=pl.CostEstimate(flops=flops, bytes_accessed=size, transcendentals=0),
        compiler_params=pltpu.CompilerParams(vmem_limit_bytes=8 << 20),
    )


def f32(*shape):
    return jax.ShapeDtypeStruct(shape, jnp.float32)


def neighbours(first, second):
    count = lax.axis_size("rows")
    results = []
    for field, step in ((first, 0), (second, 1)):
        pairs = []
        for core in range(2):
            pairs += [(2 * i + core, 2 * i + 2 + core) for i in range((core + step + 1) % 2, count - 1, 2)]
        results.append(lax.ppermute(field, ("rows", "core"), pairs + [(b, a) for a, b in pairs]))
    return results


def steps(z_blocks, z_cols, z_count, h_blocks, h_cols, h_count, panel):
    q = lax.axis_index("core")
    z = z_blocks.reshape(1024, 256)
    h = h_blocks.reshape(1024, 256)
    hbm = pl.BlockSpec(memory_space=pltpu.HBM)
    operands = (z_cols.reshape(HB), z_count, h_cols.reshape(HB), h_count, z)
    mine = pl.pallas_call(
        stage_kernel,
        out_shape=f32(1032, 256),
        in_specs=[hbm] * 5,
        out_specs=VMEM,
        scratch_shapes=[pltpu.SMEM((HB,), jnp.int32)] * 4 + [pltpu.SemaphoreType.DMA((5,))],
        compiler_params=pltpu.CompilerParams(vmem_limit_bytes=4 << 20),
        name="stage",
    )(*(pltpu.with_memory_space_constraint(a, pltpu.HBM) for a in operands))
    mine, panel, h = lax.optimization_barrier((mine, panel, h))

    swap = [(0, 1), (1, 0)]
    x = lax.dynamic_slice_in_dim(jnp.swapaxes(panel, 1, 2), q * 32, 32, axis=1)
    x_first, x_second = neighbours(x, x)
    theirs = lax.ppermute(mine, "core", swap)
    h_theirs = lax.ppermute(h, "core", swap)

    def forward(line, first, own, second, blocks):
        body = lambda *refs: forward_kernel(line, len(blocks) == 4, *refs)
        operands = (first, own, second, mine, theirs, *blocks)
        parts = call(body, f32(4, HB, 32, 256), len(operands), 1 << 28, 1 << 22)(*operands)
        return lax.all_to_all(parts, "x", 0, 0, tiled=True)

    mid = forward(0, x_first, x, x_second, (mine, theirs))
    mid = call(fold_kernel, f32(HB, 32, 256), 1, 1 << 18, 1 << 19)(mid)
    mid_first, mid_second = neighbours(mid, mid)
    half = jax.ShapeDtypeStruct((1024, 256), jnp.bfloat16)
    parts = call(split_kernel, (half,) * 8, 4, 1 << 20, 1 << 23)(h, h_theirs, mine, theirs)
    side = forward(4, mid_first, mid, mid_second, parts[:4])
    shape = f32(HB, 32, 256)
    first, own, second = call(backward_kernel, (shape, shape, shape), 7, 1 << 28, 1 << 22)(
        side, mine, theirs, *parts[4:]
    )
    first, second = neighbours(first, second)
    packed = call(pack_kernel, f32(8, 32, 128), 3, 1 << 20, 1 << 20)(own, first, second)
    arrived = lax.all_to_all(packed, ("x", "core"), 0, 0, tiled=True)
    return call(final_kernel, f32(HB, 32, 64), 1, 1 << 20, 1 << 18)(arrived)


def solution(mesh):
    grid = Mesh(mesh.devices.reshape(mesh.shape["rows"], 4, 2), ("rows", "x", "core"))
    cols = ("x", "core")
    return jax.shard_map(
        steps,
        mesh=grid,
        in_specs=(
            P("rows", cols, None, None),
            P("rows", cols),
            P("rows"),
            P("rows", cols, None, None),
            P("rows", cols),
            P("rows"),
            P("rows", None, None),
        ),
        out_specs=P("rows", cols, None),
        check_vma=False,
    )
```
